32 devices in a mesh: seq: 8 (over y, x, core), dp: 4 (over z).
Axes of the slice: x: 2, y: 2, z: 4, core: 2. Of those that a mesh axis runs over, the one named last changes fastest.
Arguments:
- tokens: bfloat16 [4, 2048, 2048], P('dp', 'seq'), may hold values from -6 to 6
- w_qkv: bfloat16 [2048, 3, 1024], P('seq'), may hold values from -0.125 to 0.125
- weight_table: float32 [16, 8], replicated, may hold values from 0.3 to 3
- weight_index: int32 [4, 16, 4], P('dp', 'seq'), may hold values from 0 to 15
- cotangent: bfloat16 [4, 2048, 1024], P('dp', 'seq'), may hold values from -6 to 6
Outputs:
- attn_out: bfloat16 [4, 2048, 1024], P('dp', 'seq')
- grad_w: float32 [2048, 3, 1024], P('seq')
The draws below stay inside these ranges and needn't reach their ends.
All inputs are finite; a program needn't handle non-finite values.
Results may differ from the reference program's by a relative error of at most 0.02.
Values may be sent and summed in bfloat16 or wider, within the bound.
A program may use at most 128 MiB of HBM per device.

```python
import math
import jax
import jax.numpy as jnp
from jax import lax

D = 2048
HEADS = 8
HEAD = 128
TOK_DEV = 256
QB = 128
NW = 16
HD = 1024
DOCS = 4
LEN = 2048
TREE = 3
N_SEQ = 8


def plant(values, rng, least, high):
    longest = values.shape.index(max(values.shape))
    spots = []
    for shift in (0, 1):
        where = [jax.random.randint(jax.random.fold_in(rng, axis), (), 0, length) for axis, length in enumerate(values.shape)]
        where[longest] = (where[longest] + shift) % values.shape[longest]
        spots.append(tuple(where))
    return values.at[spots[0]].set(least).at[spots[1]].set(high)


def spiked(result, own_key, source, target, blocks, factor):
    def block_of(axis_at):
        return (jnp.arange(result.shape[axis_at]) // (result.shape[axis_at] // blocks)).reshape((-1,) + (1,) * (result.ndim - 1 - axis_at))

    first = jax.random.permutation(own_key, blocks)[block_of(target)]
    second = (block_of(target) + blocks // 2) % blocks
    return jnp.where((block_of(source) == first) | (block_of(source) == second), factor * result, result)


def shard_levels(own_key, extent, split, least, largest):
    gain, own = 1.0, jax.random.fold_in(own_key, 6)
    for dim, shards_of in split:
        heights = jnp.exp(jax.random.uniform(jax.random.fold_in(own, dim), (shards_of,), jnp.float32, least / len(split), largest / len(split)))
        gain = gain * jnp.repeat(heights, extent[dim] // shards_of).reshape([-1 if axis == dim else 1 for axis in range(len(extent))])
    return gain


def scatter_about(stream_key, shape, scale, reach, cuts=(), dtype=jnp.bfloat16):
    drawn = jax.random.normal(stream_key, shape, jnp.float32) * scale
    if len(cuts) > 0:
        drawn = shard_levels(stream_key, shape, cuts, -0.22, 0.18) * drawn
    return jnp.clip(drawn, min=-reach, max=reach).astype(dtype)


def noise_with(key, shape, width, reach, split, heavy, kind=jnp.bfloat16):
    result = width * jax.random.normal(key, shape, jnp.float32)
    if split:
        result = result * shard_levels(key, shape, split, -0.22, 0.18)
    return jnp.clip(spiked(result, jax.random.fold_in(key, 3), *heavy), -reach, reach).astype(kind)


def setup_inputs(seed: int = 0) -> dict:
    streams_of = jax.random.split(jax.random.key(seed), 6)
    tokens = noise_with(streams_of[0], (DOCS, LEN, D), 1.0, 6.0, ((0, 4), (1, 8)), (1, 2, 8, 2.0))
    w_qkv = scatter_about(streams_of[1], (D, 3, HD), D ** -0.5, 0.125, ((0, 8),))
    weight_table = jnp.clip(jnp.exp(jax.random.uniform(streams_of[2], (NW, HEADS), jnp.float32, math.log(0.3), math.log(3.0))), 0.3, 3.0)
    weight_index = plant(jax.random.randint(streams_of[3], (DOCS, LEN // QB, TREE + 1), 0, NW), jax.random.fold_in(streams_of[3], 1), 0, NW - 1).astype(jnp.int32)
    cotangent = scatter_about(streams_of[4], (DOCS, LEN, HD), 1.0, 6.0, ((0, 4), (1, 8)))
    return {"tokens": tokens, "w_qkv": w_qkv, "weight_table": weight_table, "weight_index": weight_index, "cotangent": cotangent}


def product(pattern, left_op, right_op):
    return jnp.einsum(pattern, left_op.astype(jnp.float32), right_op.astype(jnp.float32))

def block_pass(queries, keys_bf, values_bf, upstream, local_scale, level_coef, level_states):
    block_len = queries.shape[0]
    causal = jnp.arange(block_len)[:, None] >= jnp.arange(block_len)[None, :]
    row_scale = jnp.transpose(local_scale)[:, :, None]
    raw_scores = product('thd,shd->hts', queries, keys_bf)
    scores = jnp.where(causal[None], raw_scores * row_scale, 0.0).astype(jnp.bfloat16)
    local_out = product('hts,she->the', scores, values_bf)
    far_terms = product('thd,hdle->thle', queries, level_states)
    attended = (local_out + lax.optimization_barrier(jnp.sum(far_terms * level_coef[..., None], axis=2))).astype(jnp.bfloat16)
    raw_grads = product('the,she->hts', upstream, values_bf)
    dscores = jnp.where(causal[None], raw_grads * row_scale, 0.0).astype(jnp.bfloat16)
    far_grads = product('the,hdle->thld', upstream, level_states)
    grad_q = product('hts,shd->thd', dscores, keys_bf) + lax.optimization_barrier(jnp.sum(far_grads * level_coef[..., None], axis=2))
    grad_k = product('hts,thd->shd', dscores, queries)
    grad_v = product('hts,the->she', scores, upstream)
    scaled = (queries.astype(jnp.float32)[:, :, None, :] * level_coef[..., None]).astype(jnp.bfloat16)
    level_grads = product('thld,the->hlde', scaled, upstream)
    return (attended.reshape(block_len, -1), grad_q, grad_k, grad_v, level_grads)

def one_document(inputs, chosen, upstream_all, flat_weights, weight_table):
    block_count = N_SEQ
    block_len = TOK_DEV
    head_count = HEADS
    head_dim = HEAD
    inner_width = HEADS * HEAD
    projected = jnp.dot(inputs, flat_weights, preferred_element_type=jnp.float32).astype(jnp.bfloat16)
    projected = projected.reshape(block_count, block_len, 3, head_count, head_dim)
    queries = projected[:, :, 0]
    keys_bf = projected[:, :, 1]
    values_bf = projected[:, :, 2]
    weights_tok = jnp.repeat(weight_table[chosen], QB, axis=0)
    weights_tok = weights_tok.reshape(block_count, block_len, TREE + 1, head_count)
    states = product('pshd,pshe->phde', keys_bf, values_bf)
    block_ids = jnp.arange(block_count)
    level_list = []
    flag_list = []
    for level_no in range(1, TREE + 1):
        half_span = 2 ** (level_no - 1)
        grouped = states.reshape(block_count // (2 * half_span), 2, half_span, head_count, head_dim, head_dim)
        left_sum = lax.optimization_barrier(jnp.sum(grouped[:, 0], axis=1))
        level_list.append(jnp.repeat(left_sum, 2 * half_span, axis=0))
        flag_list.append((block_ids // half_span % 2).astype(jnp.float32) / math.sqrt(head_dim * half_span * block_len))
    level_states = jnp.stack(level_list, axis=3).astype(jnp.bfloat16)
    scale_level = jnp.stack(flag_list, axis=1)
    level_coef = jnp.transpose(weights_tok[:, :, 1:], (0, 1, 3, 2)) * scale_level[:, None, None, :]
    local_scale = weights_tok[:, :, 0] / math.sqrt(head_dim * block_len)
    upstream = upstream_all.reshape(block_count, block_len, head_count, head_dim)
    results = lax.map(lambda pieces: block_pass(*pieces), (queries, keys_bf, values_bf, upstream, local_scale, level_coef, level_states))
    level_grads = results[4]
    running = jnp.zeros((block_count, head_count, head_dim, head_dim), jnp.float32)
    for level_no in range(1, TREE + 1):
        half_span = 2 ** (level_no - 1)
        grouped = level_grads[:, :, level_no - 1].reshape(block_count // (2 * half_span), 2, half_span, head_count, head_dim, head_dim)
        right_sum = lax.optimization_barrier(jnp.sum(grouped[:, 1], axis=1))
        placed = jnp.stack([right_sum, jnp.zeros_like(right_sum)], axis=1)
        placed = jnp.broadcast_to(placed[:, :, None], (block_count // (2 * half_span), 2, half_span, head_count, head_dim, head_dim))
        running = running + placed.reshape(block_count, head_count, head_dim, head_dim)
    state_grads = running.astype(jnp.bfloat16)
    grad_k = results[2] + product('pshe,phde->pshd', values_bf, state_grads)
    grad_v = results[3] + product('pshd,phde->pshe', keys_bf, state_grads)
    qkv_grads = jnp.stack([results[1], grad_k, grad_v], axis=2).astype(jnp.bfloat16)
    qkv_grads = qkv_grads.reshape(block_count, block_len, 3 * inner_width)
    attended = results[0].reshape(block_count * block_len, inner_width)
    return (attended, qkv_grads)

def reference(tokens, w_qkv, weight_table, weight_index, cotangent):
    flat_weights = w_qkv.reshape(D, 3 * HEADS * HEAD)

    def per_doc(running, pieces):
        inputs, chosen, upstream = pieces
        attended, qkv_grads = one_document(inputs, chosen, upstream, flat_weights, weight_table)

        def per_block(summed, couple):
            partial_value = jnp.dot(couple[0].T, couple[1], preferred_element_type=jnp.float32)
            rounded = lax.optimization_barrier(partial_value.astype(jnp.bfloat16))
            return (summed + rounded.astype(jnp.float32), None)
        running, ignored = lax.scan(per_block, running, (inputs.reshape(N_SEQ, TOK_DEV, D), qkv_grads))
        return (running, attended)
    anchor = jnp.zeros((D, 3 * HEADS * HEAD), jnp.float32)
    grad_w, attn_out = lax.scan(per_doc, anchor, (tokens, weight_index, cotangent))
    return (attn_out, grad_w.reshape(D, 3, HEADS * HEAD))
```

```python
import functools
import math

import jax
import jax.numpy as jnp
from jax import lax
from jax.experimental import pallas as pl
from jax.experimental.pallas import tpu as pltpu
from jax.sharding import PartitionSpec as P


def swapped(value, axis, bit):
    mask = 2**bit
    pairs = [(source, source ^ mask) for source in range(lax.axis_size(axis))]
    return lax.ppermute(value, axis, pairs)


def level_factors(weight_table, weight_index, block_len):
    table_rows = weight_table.shape[0]
    chosen = weight_index[0]
    onehot = (chosen[:, :, None] == jnp.arange(table_rows, dtype=jnp.int32)[None, None, :]).astype(
        jnp.float32
    )
    per_block = jnp.einsum("blw,wh->blh", onehot, weight_table, precision=lax.Precision.HIGHEST)
    groups = chosen.shape[0]
    spread = jnp.broadcast_to(
        per_block[:, None], (groups, block_len // groups, chosen.shape[1], weight_table.shape[1])
    )
    return spread.reshape(block_len, chosen.shape[1], weight_table.shape[1])


def make_adder(inputs, columns, shard_rows):
    flat_rows = shard_rows.reshape(shard_rows.shape[0], columns)
    return jnp.dot(inputs, flat_rows, preferred_element_type=jnp.float32)


def climb(keys_bf, values_bf, levels):
    running = jnp.einsum("shd,she->hde", keys_bf, values_bf, preferred_element_type=jnp.float32)
    partners = []
    for bit_pos in range(levels):
        partner = swapped(running.astype(jnp.bfloat16), "seq", bit_pos).astype(running.dtype)
        partners.append(partner)
        running = running + partner
    return partners


def descend(level_grads, levels, device):
    carried = [level_grads[:, bit_pos] for bit_pos in range(levels)]
    gathered = jnp.zeros_like(level_grads[:, 0])
    for bit_pos in range(levels):
        outgoing = jnp.stack(carried[bit_pos:], axis=1)
        incoming = swapped(outgoing.astype(jnp.bfloat16), "seq", bit_pos).astype(outgoing.dtype)
        keeping = (1 - device // 2**bit_pos % 2).astype(jnp.float32)
        gathered = gathered + keeping * incoming[:, 0]
        for upper in range(bit_pos + 1, levels):
            carried[upper] = carried[upper] + incoming[:, upper - bit_pos]
    return gathered


def per_device(tokens, w_qkv, weight_table, weight_index, cotangent):
    inputs = tokens[0]
    block_len = inputs.shape[0]
    inner_width = w_qkv.shape[2]
    head_count = weight_table.shape[1]
    head_dim = inner_width // head_count
    levels = lax.axis_size("seq").bit_length() - 1
    device = lax.axis_index("seq")
    projected = make_adder(
        inputs, 3 * inner_width, lax.all_gather(w_qkv, "seq", axis=0, tiled=True)
    )
    projected = projected.astype(jnp.bfloat16).reshape(block_len, 3, head_count, head_dim)
    queries = projected[:, 0]
    keys_bf = projected[:, 1]
    values_bf = projected[:, 2]
    partners = climb(keys_bf, values_bf, levels)
    level_states = jnp.stack(partners, axis=2).astype(jnp.bfloat16)
    powers = 2 ** jnp.arange(levels, dtype=jnp.int32)
    bit_flags = (device // powers % 2).astype(jnp.float32)
    halves = 2.0 ** jnp.arange(levels, dtype=jnp.float32)
    scale_level = bit_flags / jnp.sqrt(head_dim * halves * block_len)
    weights_tok = level_factors(weight_table, weight_index, block_len)
    level_coef = jnp.transpose(weights_tok[:, 1 : levels + 1, :], (0, 2, 1)) * scale_level
    local_scale = weights_tok[:, 0, :] / math.sqrt(head_dim * block_len)
    row_scale = jnp.transpose(local_scale)[:, :, None]
    causal = jnp.arange(block_len)[:, None] >= jnp.arange(block_len)[None, :]
    raw_scores = jnp.einsum("thd,shd->hts", queries, keys_bf, preferred_element_type=jnp.float32)
    scores = jnp.where(causal[None], raw_scores * row_scale, 0.0).astype(jnp.bfloat16)
    local_out = jnp.einsum("hts,she->the", scores, values_bf, preferred_element_type=jnp.float32)
    far_terms = jnp.einsum(
        "thd,hdle->thle", queries, level_states, preferred_element_type=jnp.float32
    )
    attended = local_out + jnp.sum(far_terms * level_coef[..., None], axis=2)
    attn_out = attended.astype(jnp.bfloat16).reshape(1, block_len, inner_width)
    upstream = cotangent[0].reshape(block_len, head_count, head_dim)
    raw_grads = jnp.einsum("the,she->hts", upstream, values_bf, preferred_element_type=jnp.float32)
    dscores = jnp.where(causal[None], raw_grads * row_scale, 0.0).astype(jnp.bfloat16)
    far_grads = jnp.einsum(
        "the,hdle->thld", upstream, level_states, preferred_element_type=jnp.float32
    )
    grad_q = jnp.einsum("hts,shd->thd", dscores, keys_bf, preferred_element_type=jnp.float32)
    grad_q = grad_q + jnp.sum(far_grads * level_coef[..., None], axis=2)
    grad_k = jnp.einsum("hts,thd->shd", dscores, queries, preferred_element_type=jnp.float32)
    grad_v = jnp.einsum("hts,the->she", scores, upstream, preferred_element_type=jnp.float32)
    scaled = (queries.astype(jnp.float32)[:, :, None, :] * level_coef[..., None]).astype(
        jnp.bfloat16
    )
    level_grads = jnp.einsum("thld,the->hlde", scaled, upstream, preferred_element_type=jnp.float32)
    state_grads = descend(level_grads, levels, device).astype(jnp.bfloat16)
    grad_k = grad_k + jnp.einsum(
        "she,hde->shd", values_bf, state_grads, preferred_element_type=jnp.float32
    )
    grad_v = grad_v + jnp.einsum(
        "shd,hde->she", keys_bf, state_grads, preferred_element_type=jnp.float32
    )
    qkv_grads = (
        jnp.stack([grad_q, grad_k, grad_v], axis=1)
        .astype(jnp.bfloat16)
        .reshape(block_len, 3 * inner_width)
    )
    shard_rows = w_qkv.shape[0]
    partial_value = jnp.einsum("tr,tc->rc", inputs, qkv_grads, preferred_element_type=jnp.float32)
    seq_sum = lax.psum_scatter(
        partial_value.reshape(lax.axis_size("seq") * shard_rows, 3, inner_width).astype(
            jnp.bfloat16
        ),
        "seq",
        scatter_dimension=0,
        tiled=True,
    )
    grad_w = lax.psum(seq_sum, "dp").astype(jnp.float32)
    return (attn_out, grad_w)

def head_parallel(tokens, w_qkv, weight_table, weight_index, cotangent):
    seq = lax.axis_size("seq")
    me = lax.axis_index("seq")
    inputs = tokens[0]
    block_len = inputs.shape[0]
    inner_width = w_qkv.shape[2]
    head_count = weight_table.shape[1]
    head_dim = inner_width // head_count
    own = head_count // seq
    levels = seq.bit_length() - 1
    rows = w_qkv.shape[0]
    bf = jnp.bfloat16
    f32 = jnp.float32
    every = lax.all_gather(inputs, "seq", axis=0, tiled=True)
    w_cols = w_qkv.reshape(rows, 3, seq, own * head_dim)
    w_cols = lax.all_to_all(w_cols, "seq", split_axis=2, concat_axis=0)
    w_cols = w_cols.reshape(seq * rows, 3 * own * head_dim)
    up = cotangent[0].reshape(block_len, seq, own * head_dim)
    up = lax.all_to_all(up, "seq", split_axis=1, concat_axis=0)
    up = up.reshape(seq, block_len, own, head_dim)
    chosen = lax.all_gather(weight_index[0], "seq", axis=0, tiled=True)
    table = lax.dynamic_slice_in_dim(weight_table, me * own, own, axis=1)
    lam = table[chosen]
    groups = chosen.shape[0]
    lam = jnp.repeat(lam, seq * block_len // groups, axis=0)
    lam = lam.reshape(seq, block_len, levels + 1, own)
    qkv = jnp.dot(every, w_cols, preferred_element_type=f32).astype(bf)
    qkv = qkv.reshape(seq, block_len, 3, own, head_dim)
    q, k, v = qkv[:, :, 0], qkv[:, :, 1], qkv[:, :, 2]

    def prod(pattern, a, b):
        return jnp.einsum(pattern, a, b, preferred_element_type=f32)

    states = prod("pshd,pshe->phde", k, v)
    scale0 = jnp.transpose(lam[:, :, 0], (0, 2, 1))[..., None] / math.sqrt(head_dim * block_len)
    causal = jnp.arange(block_len)[:, None] >= jnp.arange(block_len)[None, :]
    scores = jnp.where(causal, prod("pthd,pshd->phts", q, k) * scale0, 0.0).astype(bf)
    dscores = jnp.where(causal, prod("pthd,pshd->phts", up, v) * scale0, 0.0).astype(bf)
    out = prod("phts,pshe->pthe", scores, v)
    grad_q = prod("phts,pshd->pthd", dscores, k)
    grad_k = prod("phts,pthd->pshd", dscores, q)
    grad_v = prod("phts,pthe->pshe", scores, up)
    state_grads = jnp.zeros((seq, own, head_dim, head_dim), f32)
    for level in range(1, levels + 1):
        half = 2 ** (level - 1)
        shape = (seq // (2 * half), 2, half)
        tail = (own, head_dim, head_dim)
        level_state = jnp.sum(states.reshape(shape + tail)[:, 0], axis=1).astype(bf)
        coef = (lam[:, :, level] / math.sqrt(head_dim * half * block_len))[..., None]

        def right(value):
            return value.reshape(shape + value.shape[1:])[:, 1]

        q_r, up_r, coef_r = right(q), right(up), right(coef)
        far = prod("gjthd,ghde->gjthe", q_r, level_state) * coef_r
        far_q = prod("gjthe,ghde->gjthd", up_r, level_state) * coef_r
        scaled = (q_r.astype(f32) * coef_r).astype(bf)
        grads = prod("gjthd,gjthe->ghde", scaled, up_r)

        def spread(value, side):
            zero = jnp.zeros_like(value)
            pair = [value, zero] if side == 0 else [zero, value]
            return jnp.stack(pair, axis=1).reshape((seq,) + value.shape[2:])

        out = out + spread(far, 1)
        grad_q = grad_q + spread(far_q, 1)
        wide = jnp.broadcast_to(grads[:, None], (grads.shape[0], half) + tail)
        state_grads = state_grads + spread(wide, 0)
    state_grads = state_grads.astype(bf)
    grad_k = grad_k + prod("pshe,phde->pshd", v, state_grads)
    grad_v = grad_v + prod("pshd,phde->pshe", k, state_grads)
    grads = jnp.stack([grad_q, grad_k, grad_v], axis=2).astype(bf)
    grads = grads.reshape(seq * block_len, 3 * own * head_dim)
    out = out.astype(bf).reshape(seq, block_len, own * head_dim)
    out = lax.all_to_all(out, "seq", split_axis=0, concat_axis=1)
    attn_out = out.reshape(1, block_len, inner_width)
    grad_w = prod("tr,tc->rc", every, grads).astype(bf)
    grad_w = grad_w.reshape(seq, rows, 3, own * head_dim)
    grad_w = lax.all_to_all(grad_w, "seq", split_axis=0, concat_axis=2)
    grad_w = grad_w.reshape(rows, 3, inner_width)
    grad_w = lax.psum(grad_w, "dp").astype(f32)
    return (attn_out, grad_w)

def flip(index, mask):
    result = index
    for bit in (1, 2, 4):
        chosen = lax.rem(lax.div(mask, bit), 2) if not isinstance(mask, int) else mask // bit % 2
        result = result + chosen * (bit - 2 * bit * lax.rem(lax.div(index, bit), 2))
    return result


def dims(a, b, da, db):
    return lax.dot_general(a, b, (((da,), (db,)), ((), ())), preferred_element_type=jnp.float32)


def fused_kernel(
    sizes,
    tok_ref, w_ref, table_ref, index_ref, cot_ref,
    out_ref, gw_ref,
    lam_ref, xs, xt, wh, cs, lam, qkv, st, loc, outf, outb, dqkv, lvl, gl,
    gs, own, leaf, pair, pairb, fin,
    s_local, s_ws, s_wr, s_c, s_l, s_xs, s_xr, s_o, s_wz, s_war, s_wbr, s_gs, s_gr,
    s_zs, s_zar, s_zbr, s_fin,
):
    seq, dp, block, width, hd, groups, levels, parts, subs, lag = sizes
    bf = jnp.bfloat16
    f32 = jnp.float32
    me = lax.axis_index("seq")
    z = lax.axis_index("dp")
    core = lax.rem(me, 2)
    first = 2 + 2 * core
    other = 4 - 2 * core
    rows = width // seq
    part = block // parts
    piece_rows = rows // subs

    def remote(src, dst, ssem, rsem, peer):
        return pltpu.make_async_remote_copy(
            src_ref=src, dst_ref=dst, send_sem=ssem, recv_sem=rsem,
            device_id=peer, device_id_type=pl.DeviceIdType.MESH,
        )

    def lanes(index):
        return pl.ds(pl.multiple_of(index * hd, hd), hd)

    def span(index, size):
        return pl.ds(pl.multiple_of(index * size, size), size)

    barrier = pltpu.get_barrier_semaphore()
    for mask in range(1, seq):
        pl.semaphore_signal(
            barrier, inc=1, device_id={"seq": flip(me, mask)}, device_id_type=pl.DeviceIdType.MESH
        )
    for step in range(1, dp):
        pl.semaphore_signal(
            barrier, inc=1, device_id={"dp": lax.rem(z + step, dp)},
            device_id_type=pl.DeviceIdType.MESH,
        )
    for level in range(levels + 1):
        factor = jnp.float32(1 / math.sqrt(hd * block))
        if level > 0:
            bit = 2 ** (level - 1)
            flag = lax.rem(lax.div(me, bit), 2).astype(f32)
            factor = flag * jnp.float32(1 / math.sqrt(hd * bit * block))
        for g in range(groups):
            row = index_ref[g, level]
            for h in range(seq):
                lam_ref[h, pl.ds(level * groups + g, 1), :] = jnp.full(
                    (1, hd), table_ref[h, row] * factor, f32
                )
    pl.semaphore_wait(barrier, seq - 1 + dp - 1)

    inner = lax.rem(lax.div(z + 1, 2), 2) == 1
    mate = jnp.where(z < dp // 2, 1 - z, 5 - z)
    cross = 3 - z
    side = lax.div(z, 2)
    quarter = rows // dp
    half_rows = rows // 2

    def held(source, start, count):
        return pl.ds(pl.multiple_of(source * rows + start, quarter), count)

    def w_copy(mask, i):
        peer = flip(me, mask)
        near = mask == 1
        start, count = (0, rows) if near else (z * quarter, quarter)
        return remote(
            w_ref.at[i, pl.ds(pl.multiple_of(start, quarter), count), lanes(peer)],
            wh.at[held(me, start, count), pl.ds(i * hd, hd)],
            s_ws.at[0], s_wr.at[mask], {"seq": peer},
        )

    def w_arrived(mask):
        start, count = (0, rows) if mask == 1 else (z * quarter, quarter)
        piece = wh.at[held(flip(me, mask), start, count)]
        return remote(piece, piece, s_ws.at[0], s_wr.at[mask], {"seq": flip(me, mask)})

    def wa_copy(mask):
        piece = wh.at[held(flip(me, mask), z * quarter, quarter)]
        return remote(piece, piece, s_wz.at[0], s_war.at[mask], {"dp": mate})

    def wb_copy(mask):
        piece = wh.at[held(flip(me, mask), side * half_rows, half_rows)]
        return remote(piece, piece, s_wz.at[0], s_wbr.at[mask], {"dp": cross})

    def wc_copy(mask):
        piece = wh.at[held(flip(me, mask), (1 - side) * half_rows, half_rows)]
        return remote(piece, piece, s_wz.at[0], s_wbr.at[mask], {"dp": mate})

    def l_copy(mask):
        peer = flip(me, mask)
        return remote(lam_ref.at[peer], lam.at[me], s_l.at[0], s_l.at[1], {"seq": peer})

    def c_copy(mask):
        peer = flip(me, mask)
        return remote(
            cot_ref.at[:, lanes(peer)], cs.at[me], s_c.at[0], s_c.at[1], {"seq": peer}
        )

    def x_first(mask, j):
        piece = pl.ds(j * part, part)
        return remote(
            tok_ref.at[piece], xs.at[me, piece],
            s_xs.at[0], s_xr.at[mask, j], {"seq": flip(me, mask)},
        )

    def x_relay(j):
        piece = pl.ds(j * part, part)
        moved = flip(me, first)
        return remote(
            xs.at[moved, piece], xs.at[moved, piece],
            s_xs.at[0], s_xr.at[6, j], {"seq": flip(me, other)},
        )

    def x_across(mask, j):
        piece = pl.ds(j * part, part)
        moved = flip(me, mask)
        return remote(
            xs.at[moved, piece], xs.at[moved, piece],
            s_xs.at[0], s_xr.at[mask + 1, j], {"seq": flip(me, 1)},
        )

    def x_arrived(mask, j):
        piece = pl.ds(j * part, part)
        moved = flip(me, mask)
        return remote(
            xs.at[moved, piece], xs.at[moved, piece],
            s_xs.at[0], s_xr.at[mask, j], {"seq": flip(me, 1)},
        )

    def together(piece, sends, receives):
        return remote(piece, piece, sends, receives, {"seq": flip(me, 1)})

    locals_ = [
        pltpu.make_async_copy(tok_ref, xs.at[me], s_local.at[0]),
        pltpu.make_async_copy(cot_ref.at[:, lanes(me)], cs.at[me], s_local.at[1]),
        pltpu.make_async_copy(lam_ref.at[me], lam.at[me], s_local.at[2]),
    ]
    w_locals = [
        pltpu.make_async_copy(
            w_ref.at[i, :, lanes(me)], wh.at[span(me, rows), pl.ds(i * hd, hd)], s_local.at[3]
        )
        for i in range(3)
    ]
    order = (6, 7, 2, 3, 4, 5, 1)
    for mask in order:
        l_copy(mask).start()
        for i in range(3):
            w_copy(mask, i).start()
    for mask in order:
        c_copy(mask).start()
    for j in range(parts):
        for mask in (2, 4, 1):
            x_first(mask, j).start()
    for copy in locals_ + w_locals:
        copy.start()
    for copy in locals_:
        copy.wait()
    own_w = wh.at[span(me, rows)]
    pltpu.make_async_copy(own_w, own_w, s_local.at[3]).wait()
    far_masks = order[:-1]
    for mask in far_masks:
        w_arrived(mask).wait_recv()
        wa_copy(mask).start()

    def relay(j):
        x_arrived(first, j).wait_recv()
        x_relay(j).start()
        x_across(first, j).start()

    @pl.when(inner)
    def _():
        for mask in far_masks:
            wa_copy(mask).wait_recv()
            wb_copy(mask).start()
        for mask in far_masks:
            wb_copy(mask).wait_recv()
            wc_copy(mask).start()

    relay(0)

    @pl.when(jnp.logical_not(inner))
    def _():
        for mask in far_masks:
            wa_copy(mask).wait_recv()
        for mask in far_masks:
            wc_copy(mask).wait_recv()

    w_arrived(1).wait_recv()
    together(lam.at[pl.ds(0, seq - 1)], s_l.at[0], s_l.at[1]).wait_recv()
    together(cs.at[pl.ds(0, seq - 1)], s_c.at[0], s_c.at[1]).wait_recv()

    tri = lax.broadcasted_iota(jnp.int32, (block, block), 0) >= lax.broadcasted_iota(
        jnp.int32, (block, block), 1
    )

    def coef(p, level):
        pieces = []
        for g in range(groups):
            row = lam[p, pl.ds(level * groups + g, 1), :]
            pieces.append(jnp.broadcast_to(row, (block // groups, hd)))
        return jnp.concatenate(pieces, axis=0)

    def local_block(i, carry):
        half = lax.div(i, 2)
        low = lax.rem(i, 2)
        mask = jnp.where(
            half == 0, low,
            jnp.where(
                half == 1, first + low * (other - first),
                jnp.where(half == 2, 1 + other + low * (first - other), 6 + low),
            ),
        )
        p = flip(me, mask)

        @pl.when(i == 1)
        def _():
            for j in range(parts):
                x_arrived(1, j).wait_recv()

        @pl.when(i == 2)
        def _():
            for j in range(parts):
                if j > 0:
                    relay(j)
                x_arrived(other, j).wait_recv()
                x_across(other, j).start()

        @pl.when(half == 2)
        def _():
            for j in range(parts):
                x_arrived(mask, j).wait_recv()

        @pl.when(i == 6)
        def _():
            for j in range(parts):
                x_arrived(6, j).wait_recv()
                x_across(6, j).start()

        @pl.when(i == 7)
        def _():
            for j in range(parts):
                x_arrived(7, j).wait_recv()

        x = xs[p]
        proj = dims(x, wh[...], 1, 0).astype(bf)
        qkv[p] = proj
        xt[:, span(p, block)] = x.T
        q, k, v = proj[:, :hd], proj[:, hd : 2 * hd], proj[:, 2 * hd :]
        c = cs[p]
        st[p] = dims(k, v, 0, 0)
        scale = coef(p, 0)
        scale = jnp.concatenate([scale] * (block // hd), axis=1)
        scores = jnp.where(tri, dims(q, k, 1, 1) * scale, 0.0).astype(bf)
        dscores = jnp.where(tri, dims(c, v, 1, 1) * scale, 0.0).astype(bf)
        outf[p] = dims(scores, v, 1, 0)
        loc[p, :, pl.ds(0, hd)] = dims(dscores, k, 1, 0)
        loc[p, :, pl.ds(hd, hd)] = dims(dscores, q, 0, 0)
        loc[p, :, pl.ds(2 * hd, hd)] = dims(scores, c, 0, 0)
        return carry

    lax.fori_loop(0, seq, local_block, 0)

    level_sum = {}
    for level in range(1, levels + 1):
        half = 2 ** (level - 1)
        for base in range(0, seq, 2 * half):
            total = st[base]
            for j in range(1, half):
                total = total + st[base + j]
            lvl[level - 1, base] = total.astype(bf)

    def o_copy(mask):
        peer = flip(me, mask)
        return remote(
            outb.at[peer], out_ref.at[:, lanes(me)], s_o.at[0], s_o.at[1], {"seq": peer}
        )

    blank = jnp.zeros((hd, hd), bf)

    def joined(a, b, c, d):
        top = jnp.concatenate([a, b], axis=1)
        return jnp.concatenate([top, jnp.concatenate([c, d], axis=1)], axis=0)

    for level in range(1, levels + 1):
        half = 2 ** (level - 1)
        for base in range(0, seq, 2 * half):
            state = lvl[level - 1, base]
            both = joined(state, blank, blank, state.T)
            total = None
            for p in range(base + half, base + 2 * half):
                q = qkv[p, :, pl.ds(0, hd)]
                c = cs[p]
                factor = coef(p, level)
                far = dims(jnp.concatenate([q, c], axis=1), both, 1, 0)
                outf[p] += far[:, :hd] * factor
                loc[p, :, pl.ds(0, hd)] += far[:, hd:] * factor
                scaled = (q.astype(f32) * factor).astype(bf)
                grads = dims(scaled, c, 0, 0)
                total = grads if total is None else total + grads
            gl[level - 1, base] = total
    for p in range(seq):
        outb[p] = outf[p].astype(bf)
    o_local = pltpu.make_async_copy(outb.at[me], out_ref.at[:, lanes(me)], s_local.at[0])
    for p in range(seq):
        total = None
        for level in range(1, levels + 1):
            half = 2 ** (level - 1)
            if p // half % 2 == 0:
                base = p - p % (2 * half)
                term = gl[level - 1, base]
                total = term if total is None else total + term
        grads = loc[p, :, pl.ds(hd, 2 * hd)]
        if total is not None:
            g = total.astype(bf)
            both = joined(blank, g, g.T, blank)
            grads = grads + dims(qkv[p, :, pl.ds(hd, 2 * hd)], both, 1, 0)
        spot = pl.ds(p * block, block)
        dqkv[spot, pl.ds(0, hd)] = loc[p, :, pl.ds(0, hd)].astype(bf)
        dqkv[spot, pl.ds(hd, 2 * hd)] = grads.astype(bf)

    def pick(k):
        return k + jnp.where(k == 3, 1, 0) - jnp.where(k == 4, 1, 0)

    def g_copy(m):
        return remote(gs.at[m], own.at[m], s_gs.at[0], s_gr.at[m], {"seq": flip(me, m)})

    def bit_of(r):
        return pl.ds(pl.multiple_of(lax.rem(r, subs) * piece_rows, piece_rows), piece_rows)

    def za_copy(r):
        m, at = pick(lax.div(r, subs)), bit_of(r)
        return remote(own.at[m, at], leaf.at[m, at], s_zs.at[0], s_zar.at[r], {"dp": mate})

    def zb_copy(r):
        m, at = pick(lax.div(r, subs)), bit_of(r)
        return remote(pair.at[m, at], pairb.at[m, at], s_zs.at[0], s_zbr.at[r], {"dp": cross})

    def zc_copy(r):
        m, at = pick(lax.div(r, subs)), bit_of(r)
        return remote(fin.at[m, at], fin.at[m, at], s_zs.at[1], s_zar.at[r], {"dp": mate})

    def fin_copy(m, i):
        return pltpu.make_async_copy(
            fin.at[m, :, pl.ds(i * hd, hd)], gw_ref.at[i, :, lanes(flip(me, m))], s_fin.at[0]
        )

    steps = seq * subs

    def reduce_round(t, carry):
        m = pick(lax.div(t, subs))

        @pl.when((t < steps) & (lax.rem(t, subs) == 0))
        def _():
            o = flip(me, m)
            chunk = dims(xt[span(o, rows), :], dqkv[...], 1, 0).astype(bf)

            @pl.when(m == 0)
            def _():
                own[0] = chunk

            @pl.when(m > 0)
            def _():
                gs[m] = chunk
                g_copy(m).start()

            @pl.when(m == seq - 1)
            def _():
                for mask in range(1, seq):
                    o_copy(mask).start()
                o_local.start()

        @pl.when((t >= subs) & (t < steps + subs))
        def _():
            r = t - subs
            done = pick(lax.div(r, subs))
            at = bit_of(r)

            @pl.when((r >= subs) & (lax.rem(r, subs) == 0))
            def _():
                g_copy(done).wait_recv()

            @pl.when(jnp.logical_not(inner))
            def _():
                za_copy(r).start()

            @pl.when(inner)
            def _():
                za_copy(r).wait_recv()
                pair[done, at] = (own[done, at].astype(f32) + leaf[done, at].astype(f32)).astype(bf)
                zb_copy(r).start()

        @pl.when((t >= subs + lag) & inner)
        def _():
            r = t - subs - lag
            done = pick(lax.div(r, subs))
            at = bit_of(r)
            zb_copy(r).wait_recv()
            fin[done, at] = (pair[done, at].astype(f32) + pairb[done, at].astype(f32)).astype(bf)
            zc_copy(r).start()

            @pl.when(lax.rem(r, subs) == subs - 1)
            def _():
                for i in range(3):
                    fin_copy(done, i).start()

        return carry

    lax.fori_loop(0, steps + subs + lag, reduce_round, 0)

    everything = fin.at[...]

    @pl.when(jnp.logical_not(inner))
    def _():
        def collect(k, carry):
            m = pick(k)
            for b in range(subs):
                zc_copy(k * subs + b).wait_recv()
            for i in range(3):
                fin_copy(m, i).start()
            return carry

        lax.fori_loop(0, seq, collect, 0)
        together(everything, s_zs.at[0], s_zar.at[0]).wait_send()
        together(wh.at[pl.ds(0, 6 * quarter)], s_wz.at[0], s_war.at[0]).wait_send()

    @pl.when(inner)
    def _():
        together(everything, s_zs.at[0], s_zar.at[0]).wait_send()
        together(everything, s_zs.at[1], s_zar.at[0]).wait_send()
        moved = 6 * (quarter + 2 * half_rows)
        together(wh.at[pl.ds(0, moved)], s_wz.at[0], s_war.at[0]).wait_send()

    pltpu.make_async_copy(everything, everything, s_fin.at[0]).wait()
    o_local.wait()
    most = pl.ds(0, seq - 1)
    together(outb.at[most], s_o.at[0], s_o.at[1]).wait_send()
    together(outb.at[most], s_o.at[0], s_o.at[1]).wait_recv()
    together(gs.at[most], s_gs.at[0], s_gr.at[0]).wait_send()
    together(lam_ref.at[most], s_l.at[0], s_l.at[1]).wait_send()
    together(cs.at[most], s_c.at[0], s_c.at[1]).wait_send()
    together(wh.at[pl.ds(0, 6 * quarter + rows)], s_ws.at[0], s_wr.at[0]).wait_send()
    together(xs.at[most], s_xs.at[0], s_xr.at[0, 0]).wait_send()


def fused(tokens, w_qkv, weight_table, weight_index, cotangent, parts=2, subs=4, lag=3):
    seq = lax.axis_size("seq")
    dp = lax.axis_size("dp")
    block, width = tokens.shape[1:]
    inner_width = w_qkv.shape[2]
    heads = weight_table.shape[1]
    hd = inner_width // heads
    levels = seq.bit_length() - 1
    rows = w_qkv.shape[0]
    groups = weight_index.shape[1]
    bf = jnp.bfloat16
    f32 = jnp.float32
    vm = pltpu.VMEM
    dma = pltpu.SemaphoreType.DMA
    wide = (seq, rows, 3 * hd)
    out, gw = pl.pallas_call(
        functools.partial(fused_kernel, (seq, dp, block, width, hd, groups, levels, parts, subs, lag)),
        out_shape=(
            jax.ShapeDtypeStruct((block, inner_width), bf),
            jax.ShapeDtypeStruct((3, rows, inner_width), bf),
        ),
        in_specs=[
            pl.BlockSpec(memory_space=pl.ANY),
            pl.BlockSpec(memory_space=pl.ANY),
            pl.BlockSpec(memory_space=pltpu.SMEM),
            pl.BlockSpec(memory_space=pltpu.SMEM),
            pl.BlockSpec(memory_space=pl.ANY),
        ],
        out_specs=(pl.BlockSpec(memory_space=pl.ANY),) * 2,
        scratch_shapes=[
            vm((heads, (levels + 1) * groups, hd), f32),
            vm((seq, block, width), bf),
            vm((width, seq * block), bf),
            vm((width, 3 * hd), bf),
            vm((seq, block, hd), bf),
            vm((seq, (levels + 1) * groups, hd), f32),
            vm((seq, block, 3 * hd), bf),
            vm((seq, hd, hd), f32),
            vm((seq, block, 3 * hd), f32),
            vm((seq, block, hd), f32),
            vm((seq, block, hd), bf),
            vm((seq * block, 3 * hd), bf),
            vm((levels, seq, hd, hd), bf),
            vm((levels, seq, hd, hd), f32),
            vm(wide, bf), vm(wide, bf), vm(wide, bf), vm(wide, bf), vm(wide, bf), vm(wide, bf),
            dma((4,)),
            dma((1,)), dma((seq,)),
            dma((2,)),
            dma((2,)),
            dma((1,)), dma((seq, parts)),
            dma((2,)),
            dma((1,)), dma((seq,)), dma((seq,)),
            dma((1,)), dma((seq,)),
            dma((2,)), dma((seq * subs,)), dma((seq * subs,)),
            dma((1,)),
        ],
        compiler_params=pltpu.CompilerParams(
            collective_id=0, has_side_effects=True, vmem_limit_bytes=60 * 2**20
        ),
        name="fused",
    )(tokens[0], jnp.transpose(w_qkv, (1, 0, 2)), weight_table.T, weight_index[0], cotangent[0])
    return (out[None], jnp.transpose(gw, (1, 0, 2)).astype(f32))


def solution(mesh):
    def body(tokens, w_qkv, weight_table, weight_index, cotangent):
        seq, heads = mesh.shape["seq"], weight_table.shape[1]
        if seq == heads == 8 and mesh.shape["dp"] == 4:
            plan = fused
        elif heads % seq == 0:
            plan = head_parallel
        else:
            plan = per_device
        return plan(tokens, w_qkv, weight_table, weight_index, cotangent)

    return jax.shard_map(
        body,
        mesh=mesh,
        in_specs=(
            P("dp", "seq", None),
            P("seq", None, None),
            P(),
            P("dp", "seq", None),
            P("dp", "seq", None),
        ),
        out_specs=(P("dp", "seq", None), P("seq", None, None)),
        check_vma=False,
    )
```

```python
import functools
import math

import jax
import jax.numpy as jnp
from jax import lax
from jax.experimental import pallas as pl
from jax.experimental.pallas import tpu as pltpu
from jax.sharding import PartitionSpec as P


def swapped(value, axis, bit):
    mask = 2**bit
    pairs = [(source, source ^ mask) for source in range(lax.axis_size(axis))]
    return lax.ppermute(value, axis, pairs)


def level_factors(weight_table, weight_index, block_len):
    table_rows = weight_table.shape[0]
    chosen = weight_index[0]
    onehot = (chosen[:, :, None] == jnp.arange(table_rows, dtype=jnp.int32)[None, None, :]).astype(
        jnp.float32
    )
    per_block = jnp.einsum("blw,wh->blh", onehot, weight_table, precision=lax.Precision.HIGHEST)
    groups = chosen.shape[0]
    spread = jnp.broadcast_to(
        per_block[:, None], (groups, block_len // groups, chosen.shape[1], weight_table.shape[1])
    )
    return spread.reshape(block_len, chosen.shape[1], weight_table.shape[1])


def make_adder(inputs, columns, shard_rows):
    flat_rows = shard_rows.reshape(shard_rows.shape[0], columns)
    return jnp.dot(inputs, flat_rows, preferred_element_type=jnp.float32)


def climb(keys_bf, values_bf, levels):
    running = jnp.einsum("shd,she->hde", keys_bf, values_bf, preferred_element_type=jnp.float32)
    partners = []
    for bit_pos in range(levels):
        partner = swapped(running.astype(jnp.bfloat16), "seq", bit_pos).astype(running.dtype)
        partners.append(partner)
        running = running + partner
    return partners


def descend(level_grads, levels, device):
    carried = [level_grads[:, bit_pos] for bit_pos in range(levels)]
    gathered = jnp.zeros_like(level_grads[:, 0])
    for bit_pos in range(levels):
        outgoing = jnp.stack(carried[bit_pos:], axis=1)
        incoming = swapped(outgoing.astype(jnp.bfloat16), "seq", bit_pos).astype(outgoing.dtype)
        keeping = (1 - device // 2**bit_pos % 2).astype(jnp.float32)
        gathered = gathered + keeping * incoming[:, 0]
        for upper in range(bit_pos + 1, levels):
            carried[upper] = carried[upper] + incoming[:, upper - bit_pos]
    return gathered


def per_device(tokens, w_qkv, weight_table, weight_index, cotangent):
    inputs = tokens[0]
    block_len = inputs.shape[0]
    inner_width = w_qkv.shape[2]
    head_count = weight_table.shape[1]
    head_dim = inner_width // head_count
    levels = lax.axis_size("seq").bit_length() - 1
    device = lax.axis_index("seq")
    projected = make_adder(
        inputs, 3 * inner_width, lax.all_gather(w_qkv, "seq", axis=0, tiled=True)
    )
    projected = projected.astype(jnp.bfloat16).reshape(block_len, 3, head_count, head_dim)
    queries = projected[:, 0]
    keys_bf = projected[:, 1]
    values_bf = projected[:, 2]
    partners = climb(keys_bf, values_bf, levels)
    level_states = jnp.stack(partners, axis=2).astype(jnp.bfloat16)
    powers = 2 ** jnp.arange(levels, dtype=jnp.int32)
    bit_flags = (device // powers % 2).astype(jnp.float32)
    halves = 2.0 ** jnp.arange(levels, dtype=jnp.float32)
    scale_level = bit_flags / jnp.sqrt(head_dim * halves * block_len)
    weights_tok = level_factors(weight_table, weight_index, block_len)
    level_coef = jnp.transpose(weights_tok[:, 1 : levels + 1, :], (0, 2, 1)) * scale_level
    local_scale = weights_tok[:, 0, :] / math.sqrt(head_dim * block_len)
    row_scale = jnp.transpose(local_scale)[:, :, None]
    causal = jnp.arange(block_len)[:, None] >= jnp.arange(block_len)[None, :]
    raw_scores = jnp.einsum("thd,shd->hts", queries, keys_bf, preferred_element_type=jnp.float32)
    scores = jnp.where(causal[None], raw_scores * row_scale, 0.0).astype(jnp.bfloat16)
    local_out = jnp.einsum("hts,she->the", scores, values_bf, preferred_element_type=jnp.float32)
    far_terms = jnp.einsum(
        "thd,hdle->thle", queries, level_states, preferred_element_type=jnp.float32
    )
    attended = local_out + jnp.sum(far_terms * level_coef[..., None], axis=2)
    attn_out = attended.astype(jnp.bfloat16).reshape(1, block_len, inner_width)
    upstream = cotangent[0].reshape(block_len, head_count, head_dim)
    raw_grads = jnp.einsum("the,she->hts", upstream, values_bf, preferred_element_type=jnp.float32)
    dscores = jnp.where(causal[None], raw_grads * row_scale, 0.0).astype(jnp.bfloat16)
    far_grads = jnp.einsum(
        "the,hdle->thld", upstream, level_states, preferred_element_type=jnp.float32
    )
    grad_q = jnp.einsum("hts,shd->thd", dscores, keys_bf, preferred_element_type=jnp.float32)
    grad_q = grad_q + jnp.sum(far_grads * level_coef[..., None], axis=2)
    grad_k = jnp.einsum("hts,thd->shd", dscores, queries, preferred_element_type=jnp.float32)
    grad_v = jnp.einsum("hts,the->she", scores, upstream, preferred_element_type=jnp.float32)
    scaled = (queries.astype(jnp.float32)[:, :, None, :] * level_coef[..., None]).astype(
        jnp.bfloat16
    )
    level_grads = jnp.einsum("thld,the->hlde", scaled, upstream, preferred_element_type=jnp.float32)
    state_grads = descend(level_grads, levels, device).astype(jnp.bfloat16)
    grad_k = grad_k + jnp.einsum(
        "she,hde->shd", values_bf, state_grads, preferred_element_type=jnp.float32
    )
    grad_v = grad_v + jnp.einsum(
        "shd,hde->she", keys_bf, state_grads, preferred_element_type=jnp.float32
    )
    qkv_grads = (
        jnp.stack([grad_q, grad_k, grad_v], axis=1)
        .astype(jnp.bfloat16)
        .reshape(block_len, 3 * inner_width)
    )
    shard_rows = w_qkv.shape[0]
    partial_value = jnp.einsum("tr,tc->rc", inputs, qkv_grads, preferred_element_type=jnp.float32)
    seq_sum = lax.psum_scatter(
        partial_value.reshape(lax.axis_size("seq") * shard_rows, 3, inner_width).astype(
            jnp.bfloat16
        ),
        "seq",
        scatter_dimension=0,
        tiled=True,
    )
    grad_w = lax.psum(seq_sum, "dp").astype(jnp.float32)
    return (attn_out, grad_w)

def head_parallel(tokens, w_qkv, weight_table, weight_index, cotangent):
    seq = lax.axis_size("seq")
    me = lax.axis_index("seq")
    inputs = tokens[0]
    block_len = inputs.shape[0]
    inner_width = w_qkv.shape[2]
    head_count = weight_table.shape[1]
    head_dim = inner_width // head_count
    own = head_count // seq
    levels = seq.bit_length() - 1
    rows = w_qkv.shape[0]
    bf = jnp.bfloat16
    f32 = jnp.float32
    every = lax.all_gather(inputs, "seq", axis=0, tiled=True)
    w_cols = w_qkv.reshape(rows, 3, seq, own * head_dim)
    w_cols = lax.all_to_all(w_cols, "seq", split_axis=2, concat_axis=0)
    w_cols = w_cols.reshape(seq * rows, 3 * own * head_dim)
    up = cotangent[0].reshape(block_len, seq, own * head_dim)
    up = lax.all_to_all(up, "seq", split_axis=1, concat_axis=0)
    up = up.reshape(seq, block_len, own, head_dim)
    chosen = lax.all_gather(weight_index[0], "seq", axis=0, tiled=True)
    table = lax.dynamic_slice_in_dim(weight_table, me * own, own, axis=1)
    lam = table[chosen]
    groups = chosen.shape[0]
    lam = jnp.repeat(lam, seq * block_len // groups, axis=0)
    lam = lam.reshape(seq, block_len, levels + 1, own)
    qkv = jnp.dot(every, w_cols, preferred_element_type=f32).astype(bf)
    qkv = qkv.reshape(seq, block_len, 3, own, head_dim)
    q, k, v = qkv[:, :, 0], qkv[:, :, 1], qkv[:, :, 2]

    def prod(pattern, a, b):
        return jnp.einsum(pattern, a, b, preferred_element_type=f32)

    states = prod("pshd,pshe->phde", k, v)
    scale0 = jnp.transpose(lam[:, :, 0], (0, 2, 1))[..., None] / math.sqrt(head_dim * block_len)
    causal = jnp.arange(block_len)[:, None] >= jnp.arange(block_len)[None, :]
    scores = jnp.where(causal, prod("pthd,pshd->phts", q, k) * scale0, 0.0).astype(bf)
    dscores = jnp.where(causal, prod("pthd,pshd->phts", up, v) * scale0, 0.0).astype(bf)
    out = prod("phts,pshe->pthe", scores, v)
    grad_q = prod("phts,pshd->pthd", dscores, k)
    grad_k = prod("phts,pthd->pshd", dscores, q)
    grad_v = prod("phts,pthe->pshe", scores, up)
    state_grads = jnp.zeros((seq, own, head_dim, head_dim), f32)
    for level in range(1, levels + 1):
        half = 2 ** (level - 1)
        shape = (seq // (2 * half), 2, half)
        tail = (own, head_dim, head_dim)
        level_state = jnp.sum(states.reshape(shape + tail)[:, 0], axis=1).astype(bf)
        coef = (lam[:, :, level] / math.sqrt(head_dim * half * block_len))[..., None]

        def right(value):
            return value.reshape(shape + value.shape[1:])[:, 1]

        q_r, up_r, coef_r = right(q), right(up), right(coef)
        far = prod("gjthd,ghde->gjthe", q_r, level_state) * coef_r
        far_q = prod("gjthe,ghde->gjthd", up_r, level_state) * coef_r
        scaled = (q_r.astype(f32) * coef_r).astype(bf)
        grads = prod("gjthd,gjthe->ghde", scaled, up_r)

        def spread(value, side):
            zero = jnp.zeros_like(value)
            pair = [value, zero] if side == 0 else [zero, value]
            return jnp.stack(pair, axis=1).reshape((seq,) + value.shape[2:])

        out = out + spread(far, 1)
        grad_q = grad_q + spread(far_q, 1)
        wide = jnp.broadcast_to(grads[:, None], (grads.shape[0], half) + tail)
        state_grads = state_grads + spread(wide, 0)
    state_grads = state_grads.astype(bf)
    grad_k = grad_k + prod("pshe,phde->pshd", v, state_grads)
    grad_v = grad_v + prod("pshd,phde->pshe", k, state_grads)
    grads = jnp.stack([grad_q, grad_k, grad_v], axis=2).astype(bf)
    grads = grads.reshape(seq * block_len, 3 * own * head_dim)
    out = out.astype(bf).reshape(seq, block_len, own * head_dim)
    out = lax.all_to_all(out, "seq", split_axis=0, concat_axis=1)
    attn_out = out.reshape(1, block_len, inner_width)
    grad_w = prod("tr,tc->rc", every, grads).astype(bf)
    grad_w = grad_w.reshape(seq, rows, 3, own * head_dim)
    grad_w = lax.all_to_all(grad_w, "seq", split_axis=0, concat_axis=2)
    grad_w = grad_w.reshape(rows, 3, inner_width)
    grad_w = lax.psum(grad_w, "dp").astype(f32)
    return (attn_out, grad_w)

def flip(index, mask):
    result = index
    for bit in (1, 2, 4):
        chosen = lax.rem(lax.div(mask, bit), 2) if not isinstance(mask, int) else mask // bit % 2
        result = result + chosen * (bit - 2 * bit * lax.rem(lax.div(index, bit), 2))
    return result


def dims(a, b, da, db):
    return lax.dot_general(a, b, (((da,), (db,)), ((), ())), preferred_element_type=jnp.float32)


def fused_kernel(
    sizes,
    tok_ref, w_ref, table_ref, index_ref, cot_ref,
    out_ref, gw_ref,
    lam_ref, xs, xt, wh, cs, lam, qkv, st, loc, outf, outb, dqkv, lvl, gl,
    gs, own, leaf, pair, pairb, fin,
    s_local, s_ws, s_wr, s_c, s_l, s_xs, s_xr, s_o, s_wz, s_war, s_wbr, s_gs, s_gr,
    s_zs, s_zar, s_zbr, s_fin,
):
    seq, dp, block, width, hd, groups, levels, parts, subs, lag, ahead = sizes
    bf = jnp.bfloat16
    f32 = jnp.float32
    me = lax.axis_index("seq")
    z = lax.axis_index("dp")
    core = lax.rem(me, 2)
    first = 2 + 2 * core
    other = 4 - 2 * core
    rows = width // seq
    part = block // parts
    piece_rows = rows // subs

    def remote(src, dst, ssem, rsem, peer):
        return pltpu.make_async_remote_copy(
            src_ref=src, dst_ref=dst, send_sem=ssem, recv_sem=rsem,
            device_id=peer, device_id_type=pl.DeviceIdType.MESH,
        )

    def lanes(index):
        return pl.ds(pl.multiple_of(index * hd, hd), hd)

    def span(index, size):
        return pl.ds(pl.multiple_of(index * size, size), size)

    barrier = pltpu.get_barrier_semaphore()
    for mask in range(1, seq):
        pl.semaphore_signal(
            barrier, inc=1, device_id={"seq": flip(me, mask)}, device_id_type=pl.DeviceIdType.MESH
        )
    for step in range(1, dp):
        pl.semaphore_signal(
            barrier, inc=1, device_id={"dp": lax.rem(z + step, dp)},
            device_id_type=pl.DeviceIdType.MESH,
        )
    for level in range(levels + 1):
        factor = jnp.float32(1 / math.sqrt(hd * block))
        if level > 0:
            bit = 2 ** (level - 1)
            flag = lax.rem(lax.div(me, bit), 2).astype(f32)
            factor = flag * jnp.float32(1 / math.sqrt(hd * bit * block))
        for g in range(groups):
            row = index_ref[g, level]
            for h in range(seq):
                lam_ref[h, pl.ds(level * groups + g, 1), :] = jnp.full(
                    (1, hd), table_ref[h, row] * factor, f32
                )
    pl.semaphore_wait(barrier, seq - 1 + dp - 1)

    inner = lax.rem(lax.div(z + 1, 2), 2) == 1
    mate = jnp.where(z < dp // 2, 1 - z, 5 - z)
    cross = 3 - z
    side = lax.div(z, 2)
    quarter = rows // dp
    half_rows = rows // 2

    def held(source, start, count):
        return pl.ds(pl.multiple_of(source * rows + start, quarter), count)

    def w_copy(mask, i):
        peer = flip(me, mask)
        near = mask == 1
        start, count = (0, rows) if near else (z * quarter, quarter)
        return remote(
            w_ref.at[i, pl.ds(pl.multiple_of(start, quarter), count), lanes(peer)],
            wh.at[held(me, start, count), pl.ds(i * hd, hd)],
            s_ws.at[0], s_wr.at[mask], {"seq": peer},
        )

    def w_arrived(mask):
        start, count = (0, rows) if mask == 1 else (z * quarter, quarter)
        piece = wh.at[held(flip(me, mask), start, count)]
        return remote(piece, piece, s_ws.at[0], s_wr.at[mask], {"seq": flip(me, mask)})

    def wa_copy(mask):
        piece = wh.at[held(flip(me, mask), z * quarter, quarter)]
        return remote(piece, piece, s_wz.at[0], s_war.at[mask], {"dp": mate})

    def wb_copy(mask):
        piece = wh.at[held(flip(me, mask), side * half_rows, half_rows)]
        return remote(piece, piece, s_wz.at[0], s_wbr.at[mask], {"dp": cross})

    def wc_copy(mask):
        piece = wh.at[held(flip(me, mask), (1 - side) * half_rows, half_rows)]
        return remote(piece, piece, s_wz.at[0], s_wbr.at[mask], {"dp": mate})

    def l_copy(mask):
        peer = flip(me, mask)
        return remote(lam_ref.at[peer], lam.at[me], s_l.at[0], s_l.at[1], {"seq": peer})

    def c_copy(mask):
        peer = flip(me, mask)
        return remote(
            cot_ref.at[:, lanes(peer)], cs.at[me], s_c.at[0], s_c.at[1], {"seq": peer}
        )

    def x_first(mask, j):
        piece = pl.ds(j * part, part)
        return remote(
            tok_ref.at[piece], xs.at[me, piece],
            s_xs.at[0], s_xr.at[mask, j], {"seq": flip(me, mask)},
        )

    def x_relay(j):
        piece = pl.ds(j * part, part)
        moved = flip(me, first)
        return remote(
            xs.at[moved, piece], xs.at[moved, piece],
            s_xs.at[0], s_xr.at[6, j], {"seq": flip(me, other)},
        )

    def x_across(mask, j):
        piece = pl.ds(j * part, part)
        moved = flip(me, mask)
        return remote(
            xs.at[moved, piece], xs.at[moved, piece],
            s_xs.at[0], s_xr.at[mask + 1, j], {"seq": flip(me, 1)},
        )

    def x_arrived(mask, j):
        piece = pl.ds(j * part, part)
        moved = flip(me, mask)
        return remote(
            xs.at[moved, piece], xs.at[moved, piece],
            s_xs.at[0], s_xr.at[mask, j], {"seq": flip(me, 1)},
        )

    def together(piece, sends, receives):
        return remote(piece, piece, sends, receives, {"seq": flip(me, 1)})

    locals_ = [
        pltpu.make_async_copy(tok_ref, xs.at[me], s_local.at[0]),
        pltpu.make_async_copy(cot_ref.at[:, lanes(me)], cs.at[me], s_local.at[1]),
        pltpu.make_async_copy(lam_ref.at[me], lam.at[me], s_local.at[2]),
    ]
    w_locals = [
        pltpu.make_async_copy(
            w_ref.at[i, :, lanes(me)], wh.at[span(me, rows), pl.ds(i * hd, hd)], s_local.at[3]
        )
        for i in range(3)
    ]
    order = (6, 7, 2, 3, 4, 5, 1)
    for mask in order:
        l_copy(mask).start()
        for i in range(3):
            w_copy(mask, i).start()
    for mask in order:
        c_copy(mask).start()
    for j in range(parts):
        for mask in (2, 4, 1):
            x_first(mask, j).start()
    for copy in locals_ + w_locals:
        copy.start()
    for copy in locals_:
        copy.wait()
    own_w = wh.at[span(me, rows)]
    pltpu.make_async_copy(own_w, own_w, s_local.at[3]).wait()
    far_masks = order[:-1]
    for mask in far_masks:
        w_arrived(mask).wait_recv()
        wa_copy(mask).start()

    def relay(j):
        x_arrived(first, j).wait_recv()
        x_relay(j).start()
        x_across(first, j).start()

    @pl.when(inner)
    def _():
        for mask in far_masks:
            wa_copy(mask).wait_recv()
            wb_copy(mask).start()
        for mask in far_masks:
            wb_copy(mask).wait_recv()
            wc_copy(mask).start()

    relay(0)

    @pl.when(jnp.logical_not(inner))
    def _():
        for mask in far_masks:
            wa_copy(mask).wait_recv()
        for mask in far_masks:
            wc_copy(mask).wait_recv()

    w_arrived(1).wait_recv()
    together(lam.at[pl.ds(0, seq - 1)], s_l.at[0], s_l.at[1]).wait_recv()
    together(cs.at[pl.ds(0, seq - 1)], s_c.at[0], s_c.at[1]).wait_recv()

    tri = lax.broadcasted_iota(jnp.int32, (block, block), 0) >= lax.broadcasted_iota(
        jnp.int32, (block, block), 1
    )

    def coef(p, level):
        pieces = []
        for g in range(groups):
            row = lam[p, pl.ds(level * groups + g, 1), :]
            pieces.append(jnp.broadcast_to(row, (block // groups, hd)))
        return jnp.concatenate(pieces, axis=0)

    def local_block(i, carry):
        half = lax.div(i, 2)
        low = lax.rem(i, 2)
        mask = jnp.where(
            half == 0, low,
            jnp.where(
                half == 1, first + low * (other - first),
                jnp.where(half == 2, 1 + other + low * (first - other), 6 + low),
            ),
        )
        p = flip(me, mask)

        @pl.when(i == 1)
        def _():
            for j in range(parts):
                x_arrived(1, j).wait_recv()

        @pl.when(i == 2)
        def _():
            for j in range(parts):
                if j > 0:
                    relay(j)
                x_arrived(other, j).wait_recv()
                x_across(other, j).start()

        @pl.when(half == 2)
        def _():
            for j in range(parts):
                x_arrived(mask, j).wait_recv()

        @pl.when(i == 6)
        def _():
            for j in range(parts):
                x_arrived(6, j).wait_recv()
                x_across(6, j).start()

        @pl.when(i == 7)
        def _():
            for j in range(parts):
                x_arrived(7, j).wait_recv()

        x = xs[p]
        proj = dims(x, wh[...], 1, 0).astype(bf)
        qkv[p] = proj
        xt[:, span(p, block)] = x.T
        q, k, v = proj[:, :hd], proj[:, hd : 2 * hd], proj[:, 2 * hd :]
        c = cs[p]
        st[p] = dims(k, v, 0, 0)
        scale = coef(p, 0)
        scale = jnp.concatenate([scale] * (block // hd), axis=1)
        scores = jnp.where(tri, dims(q, k, 1, 1) * scale, 0.0).astype(bf)
        dscores = jnp.where(tri, dims(c, v, 1, 1) * scale, 0.0).astype(bf)
        outf[p] = dims(scores, v, 1, 0)
        loc[p, :, pl.ds(0, hd)] = dims(dscores, k, 1, 0)
        loc[p, :, pl.ds(hd, hd)] = dims(dscores, q, 0, 0)
        loc[p, :, pl.ds(2 * hd, hd)] = dims(scores, c, 0, 0)
        return carry

    lax.fori_loop(0, seq, local_block, 0)

    level_sum = {}
    for level in range(1, levels + 1):
        half = 2 ** (level - 1)
        for base in range(0, seq, 2 * half):
            total = st[base]
            for j in range(1, half):
                total = total + st[base + j]
            lvl[level - 1, base] = total.astype(bf)

    def o_copy(mask):
        peer = flip(me, mask)
        return remote(
            outb.at[peer], out_ref.at[:, lanes(me)], s_o.at[0], s_o.at[1], {"seq": peer}
        )

    blank = jnp.zeros((hd, hd), bf)

    def joined(a, b, c, d):
        top = jnp.concatenate([a, b], axis=1)
        return jnp.concatenate([top, jnp.concatenate([c, d], axis=1)], axis=0)

    for level in range(1, levels + 1):
        half = 2 ** (level - 1)
        for base in range(0, seq, 2 * half):
            state = lvl[level - 1, base]
            both = joined(state, blank, blank, state.T)
            total = None
            for p in range(base + half, base + 2 * half):
                q = qkv[p, :, pl.ds(0, hd)]
                c = cs[p]
                factor = coef(p, level)
                far = dims(jnp.concatenate([q, c], axis=1), both, 1, 0)
                outf[p] += far[:, :hd] * factor
                loc[p, :, pl.ds(0, hd)] += far[:, hd:] * factor
                scaled = (q.astype(f32) * factor).astype(bf)
                grads = dims(scaled, c, 0, 0)
                total = grads if total is None else total + grads
            gl[level - 1, base] = total
    for p in range(seq):
        outb[p] = outf[p].astype(bf)
    o_local = pltpu.make_async_copy(outb.at[me], out_ref.at[:, lanes(me)], s_local.at[0])
    for p in range(seq):
        total = None
        for level in range(1, levels + 1):
            half = 2 ** (level - 1)
            if p // half % 2 == 0:
                base = p - p % (2 * half)
                term = gl[level - 1, base]
                total = term if total is None else total + term
        grads = loc[p, :, pl.ds(hd, 2 * hd)]
        if total is not None:
            g = total.astype(bf)
            both = joined(blank, g, g.T, blank)
            grads = grads + dims(qkv[p, :, pl.ds(hd, 2 * hd)], both, 1, 0)
        spot = pl.ds(p * block, block)
        dqkv[spot, pl.ds(0, hd)] = loc[p, :, pl.ds(0, hd)].astype(bf)
        dqkv[spot, pl.ds(hd, 2 * hd)] = grads.astype(bf)

    def pick(k):
        return k + jnp.where(k == 3, 1, 0) - jnp.where(k == 4, 1, 0)

    def g_copy(m):
        return remote(gs.at[m], own.at[m], s_gs.at[0], s_gr.at[m], {"seq": flip(me, m)})

    def bit_of(r):
        return pl.ds(pl.multiple_of(lax.rem(r, subs) * piece_rows, piece_rows), piece_rows)

    def za_copy(r):
        m, at = pick(lax.div(r, subs)), bit_of(r)
        return remote(own.at[m, at], leaf.at[m, at], s_zs.at[0], s_zar.at[r], {"dp": mate})

    def zb_copy(r):
        m, at = pick(lax.div(r, subs)), bit_of(r)
        return remote(pair.at[m, at], pairb.at[m, at], s_zs.at[0], s_zbr.at[r], {"dp": cross})

    def zc_copy(r):
        m, at = pick(lax.div(r, subs)), bit_of(r)
        return remote(fin.at[m, at], fin.at[m, at], s_zs.at[1], s_zar.at[r], {"dp": mate})

    def fin_copy(m, i):
        return pltpu.make_async_copy(
            fin.at[m, :, pl.ds(i * hd, hd)], gw_ref.at[i, :, lanes(flip(me, m))], s_fin.at[0]
        )

    steps = seq * subs

    def make_chunk(m):
        o = flip(me, m)
        chunk = dims(xt[span(o, rows), :], dqkv[...], 1, 0).astype(bf)

        @pl.when(m == 0)
        def _():
            own[0] = chunk

        @pl.when(m > 0)
        def _():
            gs[m] = chunk
            g_copy(m).start()

        @pl.when(m == seq - 1)
        def _():
            for mask in range(1, seq):
                o_copy(mask).start()
            o_local.start()

    def prepare(k, carry):
        make_chunk(pick(k))

        @pl.when((k == 0) & jnp.logical_not(inner))
        def _():
            for r in range(subs):
                za_copy(r).start()

        return carry

    lax.fori_loop(0, ahead, prepare, 0)

    def reduce_round(r, carry):
        k = lax.div(r, subs)

        @pl.when((k < seq - ahead) & (lax.rem(r, subs) == 0))
        def _():
            make_chunk(pick(k + ahead))

        @pl.when((r >= subs) & (r < steps))
        def _():
            @pl.when(lax.rem(r, subs) == 0)
            def _():
                g_copy(pick(k)).wait_recv()

            @pl.when(jnp.logical_not(inner))
            def _():
                za_copy(r).start()

        @pl.when((r < steps) & inner)
        def _():
            done = pick(k)
            at = bit_of(r)
            za_copy(r).wait_recv()
            pair[done, at] = (own[done, at].astype(f32) + leaf[done, at].astype(f32)).astype(bf)
            zb_copy(r).start()

        @pl.when((r >= lag) & inner)
        def _():
            back = r - lag
            done = pick(lax.div(back, subs))
            at = bit_of(back)
            zb_copy(back).wait_recv()
            fin[done, at] = (pair[done, at].astype(f32) + pairb[done, at].astype(f32)).astype(bf)
            zc_copy(back).start()

            @pl.when(lax.rem(back, subs) == subs - 1)
            def _():
                for i in range(3):
                    fin_copy(done, i).start()

        return carry

    lax.fori_loop(0, steps + lag, reduce_round, 0)

    everything = fin.at[...]

    @pl.when(jnp.logical_not(inner))
    def _():
        def collect(k, carry):
            m = pick(k)
            for b in range(subs):
                zc_copy(k * subs + b).wait_recv()
            for i in range(3):
                fin_copy(m, i).start()
            return carry

        lax.fori_loop(0, seq, collect, 0)
        together(everything, s_zs.at[0], s_zar.at[0]).wait_send()
        together(wh.at[pl.ds(0, 6 * quarter)], s_wz.at[0], s_war.at[0]).wait_send()

    @pl.when(inner)
    def _():
        together(everything, s_zs.at[0], s_zar.at[0]).wait_send()
        together(everything, s_zs.at[1], s_zar.at[0]).wait_send()
        moved = 6 * (quarter + 2 * half_rows)
        together(wh.at[pl.ds(0, moved)], s_wz.at[0], s_war.at[0]).wait_send()

    pltpu.make_async_copy(everything, everything, s_fin.at[0]).wait()
    o_local.wait()
    most = pl.ds(0, seq - 1)
    together(outb.at[most], s_o.at[0], s_o.at[1]).wait_send()
    together(outb.at[most], s_o.at[0], s_o.at[1]).wait_recv()
    together(gs.at[most], s_gs.at[0], s_gr.at[0]).wait_send()
    together(lam_ref.at[most], s_l.at[0], s_l.at[1]).wait_send()
    together(cs.at[most], s_c.at[0], s_c.at[1]).wait_send()
    together(wh.at[pl.ds(0, 6 * quarter + rows)], s_ws.at[0], s_wr.at[0]).wait_send()
    together(xs.at[most], s_xs.at[0], s_xr.at[0, 0]).wait_send()


def fused(tokens, w_qkv, weight_table, weight_index, cotangent, parts=2, subs=4, lag=3, ahead=3):
    seq = lax.axis_size("seq")
    dp = lax.axis_size("dp")
    block, width = tokens.shape[1:]
    inner_width = w_qkv.shape[2]
    heads = weight_table.shape[1]
    hd = inner_width // heads
    levels = seq.bit_length() - 1
    rows = w_qkv.shape[0]
    groups = weight_index.shape[1]
    bf = jnp.bfloat16
    f32 = jnp.float32
    vm = pltpu.VMEM
    dma = pltpu.SemaphoreType.DMA
    wide = (seq, rows, 3 * hd)
    out, gw = pl.pallas_call(
        functools.partial(fused_kernel, (seq, dp, block, width, hd, groups, levels, parts, subs, lag, ahead)),
        out_shape=(
            jax.ShapeDtypeStruct((block, inner_width), bf),
            jax.ShapeDtypeStruct((3, rows, inner_width), bf),
        ),
        in_specs=[
            pl.BlockSpec(memory_space=pl.ANY),
            pl.BlockSpec(memory_space=pl.ANY),
            pl.BlockSpec(memory_space=pltpu.SMEM),
            pl.BlockSpec(memory_space=pltpu.SMEM),
            pl.BlockSpec(memory_space=pl.ANY),
        ],
        out_specs=(pl.BlockSpec(memory_space=pl.ANY),) * 2,
        scratch_shapes=[
            vm((heads, (levels + 1) * groups, hd), f32),
            vm((seq, block, width), bf),
            vm((width, seq * block), bf),
            vm((width, 3 * hd), bf),
            vm((seq, block, hd), bf),
            vm((seq, (levels + 1) * groups, hd), f32),
            vm((seq, block, 3 * hd), bf),
            vm((seq, hd, hd), f32),
            vm((seq, block, 3 * hd), f32),
            vm((seq, block, hd), f32),
            vm((seq, block, hd), bf),
            vm((seq * block, 3 * hd), bf),
            vm((levels, seq, hd, hd), bf),
            vm((levels, seq, hd, hd), f32),
            vm(wide, bf), vm(wide, bf), vm(wide, bf), vm(wide, bf), vm(wide, bf), vm(wide, bf),
            dma((4,)),
            dma((1,)), dma((seq,)),
            dma((2,)),
            dma((2,)),
            dma((1,)), dma((seq, parts)),
            dma((2,)),
            dma((1,)), dma((seq,)), dma((seq,)),
            dma((1,)), dma((seq,)),
            dma((2,)), dma((seq * subs,)), dma((seq * subs,)),
            dma((1,)),
        ],
        compiler_params=pltpu.CompilerParams(
            collective_id=0, has_side_effects=True, vmem_limit_bytes=60 * 2**20
        ),
        name="fused",
    )(tokens[0], jnp.transpose(w_qkv, (1, 0, 2)), weight_table.T, weight_index[0], cotangent[0])
    return (out[None], jnp.transpose(gw, (1, 0, 2)).astype(f32))


def solution(mesh):
    def body(tokens, w_qkv, weight_table, weight_index, cotangent):
        seq, heads = mesh.shape["seq"], weight_table.shape[1]
        if seq == heads == 8 and mesh.shape["dp"] == 4:
            plan = fused
        elif heads % seq == 0:
            plan = head_parallel
        else:
            plan = per_device
        return plan(tokens, w_qkv, weight_table, weight_index, cotangent)

    return jax.shard_map(
        body,
        mesh=mesh,
        in_specs=(
            P("dp", "seq", None),
            P("seq", None, None),
            P(),
            P("dp", "seq", None),
            P("dp", "seq", None),
        ),
        out_specs=(P("dp", "seq", None), P("seq", None, None)),
        check_vma=False,
    )
```
